32 devices in a mesh: seg: 2 (over y), row: 4 (over x, core), col: 4 (over z).
Axes of the slice: x: 2, y: 2, z: 4, core: 2. Of those that a mesh axis runs over, the one named last changes fastest.
Arguments:
- raw_traces: bfloat16 [8192, 16, 256], P(('seg', 'row', 'col')), parts along dimension 0, may hold values from -6 to 6
- channel_pick: int32 [4096], P(('seg', 'row', 'col')), parts along dimension 0, may hold values from 0 to 4095, as said below
- clip_mask: int32 [4096, 16], P(('seg', 'row', 'col')), parts along dimension 0, may hold values 0 or 1
Outputs:
- correlations: bfloat16 [4096, 2048, 128], P(('seg', 'row'), 'col'), parts along dimension 0
The draws below stay inside these ranges and needn't reach their ends.
There are 2 independent parts, one for each index of `seg`. The reference program is written for one: setup_inputs(seed, part) draws one part's arguments, and reference() takes and returns one part's arrays. A program takes and returns all parts, laid end to end along the dimension named above; each array names one. Nothing has to cross between parts.
Inputs may be any that keep to these rules, and one draw needn't show every extreme that they name: `channel_pick`: entry j is 2j or 2j+1; entry 0 is even and entry 2047 is odd.
All inputs are finite; a program needn't handle non-finite values. No bound on the sum of `clip_mask` on one device may be relied on, other than what follows from the above.
Results may differ from the reference program's by a relative error of at most 0.0057.
Values may be sent and summed in bfloat16 or wider, within the bound.
A program may use at most 576 MiB of HBM per device.

```python
import math
import jax
import jax.numpy as jnp
from jax import lax

C = 2048
W = 16
S = 256
L = 128
K = 128
CR = 4096
TILE = 512
N_ROW = 4


def draw_channel_pick(key, part):
    bits = jax.random.randint(key, (C,), 0, 2, dtype=jnp.int32)
    position = jnp.arange(C, dtype=jnp.int32)
    bits = jnp.where(position == 0, 0, jnp.where(position == C - 1, 1, bits))
    return 2 * position + bits


def set_ends(drawn, key, smallest, largest):
    extent = drawn.shape
    place = [jax.random.randint(jax.random.fold_in(key, axis), (), 0, extent[axis]) for axis in range(len(extent))]
    drawn = drawn.at[tuple(place)].set(smallest)
    longest = extent.index(max(extent))
    place[longest] = (place[longest] + 1) % extent[longest]
    return drawn.at[tuple(place)].set(largest)


def steps_of(own_key, extent, split, low, high):
    gain, own = 1.0, jax.random.fold_in(own_key, 6)
    for dim, parts in split:
        steps = jnp.exp(jax.random.uniform(jax.random.fold_in(own, dim), (parts,), jnp.float32, low / len(split), high / len(split)))
        gain = gain * jnp.repeat(steps, extent[dim] // parts).reshape([-1 if axis == dim else 1 for axis in range(len(extent))])
    return gain


def scatter_about(key, shape, scale, reach, pieces=(), kind=jnp.bfloat16):
    result = jax.random.normal(key, shape, jnp.float32) * scale
    if len(pieces) > 0:
        result = steps_of(key, shape, pieces, -0.22, 0.18) * result
    return jnp.clip(result, min=-reach, max=reach).astype(kind)


def setup_inputs(seed: int = 0, part: int = 0) -> dict:
    key_list = jax.random.split(jax.random.key(seed), 4)
    part_keys = jax.random.split(jax.random.fold_in(key_list[3], part), 4)
    return {
        "raw_traces": scatter_about(part_keys[0], (CR, W, S), 1.0, 6.0, ((0, 16),)),
        "channel_pick": draw_channel_pick(jax.random.fold_in(jax.random.fold_in(key_list[3], part), 71), part),
        "clip_mask": set_ends((jax.random.randint(part_keys[2], (C, W), 0, 8) < 7).astype(jnp.int32), jax.random.fold_in(part_keys[2], 1), 0, 1),
    }


def whiten_block(picked, keep):
    samples = picked.shape[2]
    half = samples // 2
    pos = jnp.arange(samples, dtype=jnp.int32)
    freq = jnp.arange(1, half + 1, dtype=jnp.int32)
    phase = pos[:, None] * freq[None, :] % samples
    angle = phase.astype(jnp.float32) * (2.0 * math.pi / samples)
    table = jnp.concatenate([jnp.cos(angle), -jnp.sin(angle)], axis=1)
    flat = picked.astype(jnp.float32).reshape(-1, samples)
    spec = jnp.dot(flat, table, precision=lax.Precision.HIGHEST, preferred_element_type=jnp.float32)
    real_part = spec[:, :half]
    imag_part = spec[:, half:]
    power = real_part * real_part + imag_part * imag_part
    gap = jnp.abs(freq[:, None] - freq[None, :])
    band = jnp.where(gap <= 2, 0.2, 0.0).astype(jnp.float32)
    smooth = jnp.dot(power, band, precision=lax.Precision.HIGHEST, preferred_element_type=jnp.float32)
    denom = jnp.sqrt(smooth + 0.1 * lax.optimization_barrier(jnp.mean(power, axis=1, keepdims=True)) + 1e-06)
    weight = keep.reshape(-1, 1).astype(jnp.float32) / denom
    whitened = jnp.concatenate([real_part * weight, imag_part * weight], axis=1)
    return whitened.astype(jnp.bfloat16).reshape(picked.shape[0], picked.shape[1], samples)

def lag_tables(half, samples, lags, windows):
    freq = jnp.arange(1, half + 1, dtype=jnp.int32)
    shift = jnp.arange(lags, dtype=jnp.int32) - lags // 2
    phase = freq[:, None] * shift[None, :] % samples
    angle = phase.astype(jnp.float32) * (2.0 * math.pi / samples)
    scale = 1.0 / math.sqrt(windows * half)
    return (jnp.cos(angle) * scale, jnp.sin(angle) * scale)

def reference(raw_traces, channel_pick, clip_mask):
    picked = raw_traces[channel_pick]
    spectra = whiten_block(picked, clip_mask)
    stacked = spectra.astype(jnp.float32).reshape(C, W, 2, K)
    rotated = jnp.concatenate([-spectra[:, :, K:], spectra[:, :, :K]], axis=2).astype(jnp.float32).reshape(C, W, 2, K)
    cos_table, sin_table = lag_tables(K, S, L, W)
    columns = jnp.arange(C, dtype=jnp.int32)

    def one_block(start):
        rows = lax.dynamic_slice_in_dim(stacked, start, TILE, 0)
        cross_re = jnp.einsum('iwpk,jwpk->ijk', rows, stacked, precision=lax.Precision.HIGHEST)
        cross_im = jnp.einsum('iwpk,jwpk->ijk', rows, rotated, precision=lax.Precision.HIGHEST)
        lagged = jnp.dot(cross_re.reshape(-1, K), cos_table, precision=lax.Precision.HIGHEST, preferred_element_type=jnp.float32)
        lagged = lagged - jnp.dot(cross_im.reshape(-1, K), sin_table, precision=lax.Precision.HIGHEST, preferred_element_type=jnp.float32)
        lagged = lagged.reshape(TILE, C, L)
        row_ids = start + jnp.arange(TILE, dtype=jnp.int32)
        same = row_ids[:, None] == columns[None, :]
        return jnp.where(same[:, :, None], 0.0, lagged).astype(jnp.bfloat16)
    starts = jnp.arange(N_ROW, dtype=jnp.int32) * TILE
    blocks = lax.map(one_block, starts)
    return blocks.reshape(C, C, L)
```

```python
import functools
import math

import jax
import jax.numpy as jnp
from jax import lax
from jax.experimental import pallas as pl
from jax.experimental.pallas import tpu as pltpu
from jax.sharding import PartitionSpec as P

L = 128
LANES = 128
PAD = 8
FLIP = True
UNROLL1 = 4
UNROLL2 = 4


def whiten_block(picked, keep):
    samples = picked.shape[2]
    half = samples // 2
    pos = jnp.arange(samples, dtype=jnp.int32)
    freq = jnp.arange(1, half + 1, dtype=jnp.int32)
    phase = pos[:, None] * freq[None, :] % samples
    angle = phase.astype(jnp.float32) * (2.0 * math.pi / samples)
    table = jnp.concatenate([jnp.cos(angle), -jnp.sin(angle)], axis=1)
    flat = picked.astype(jnp.float32).reshape(-1, samples)
    spec = jnp.dot(flat, table, precision=lax.Precision.HIGHEST, preferred_element_type=jnp.float32)
    real_part = spec[:, :half]
    imag_part = spec[:, half:]
    power = real_part * real_part + imag_part * imag_part
    gap = jnp.abs(freq[:, None] - freq[None, :])
    band = jnp.where(gap <= 2, 0.2, 0.0).astype(jnp.float32)
    smooth = jnp.dot(
        power, band, precision=lax.Precision.HIGHEST, preferred_element_type=jnp.float32
    )
    denom = jnp.sqrt(smooth + 0.1 * jnp.mean(power, axis=1, keepdims=True) + 1e-06)
    weight = keep.reshape(-1, 1).astype(jnp.float32) / denom
    whitened = jnp.concatenate([real_part * weight, imag_part * weight], axis=1)
    return whitened.astype(jnp.bfloat16).reshape(picked.shape[0], picked.shape[1], samples)


def lag_table(half, samples, lags, windows):
    freq = jnp.arange(1, half + 1, dtype=jnp.int32)
    shift = jnp.arange(lags, dtype=jnp.int32) - lags // 2
    phase = freq[:, None] * shift[None, :] % samples
    angle = phase.astype(jnp.float32) * (2.0 * math.pi / samples)
    scale = 1.0 / math.sqrt(windows * half)
    both = jnp.concatenate([jnp.cos(angle) * scale, -jnp.sin(angle) * scale], axis=0)
    return both.astype(jnp.bfloat16)


def pair_kernel(offs_ref, first_ref, second_ref, table_ref, out_ref, cross_ref):
    groups, half, depth, wide = second_ref.shape
    rows = first_ref.shape[-1]
    both = 2 * half
    stride = both + PAD
    windows = depth // 2

    def spectra(k, carry):
        a = first_ref[k]
        turned = jnp.concatenate([a[windows:], -a[:windows]], axis=0)
        b = jnp.concatenate([second_ref[g, k] for g in range(groups)], axis=1)
        for part, lhs in enumerate((a, turned)):
            res = lax.dot_general(
                lhs, b, (((0,), (0,)), ((), ())), preferred_element_type=jnp.float32
            )
            for g in range(groups):
                cross_ref[g, pl.ds(part * half + k, rows, stride=stride), :] = res[
                    :, g * wide : (g + 1) * wide
                ]
        return carry

    lax.fori_loop(0, half, spectra, 0, unroll=UNROLL1)

    row0 = offs_ref[0] + pl.program_id(0) * rows
    col0 = offs_ref[1] + pl.program_id(1) * (groups * wide)
    lags = table_ref.shape[0] if FLIP else table_ref.shape[1]
    place = lax.broadcasted_iota(jnp.int32, (groups * wide, lags), 0) + (col0 - row0)

    def lagged(i, carry):
        start = pl.multiple_of(i * stride, 8)
        x = jnp.concatenate(
            [cross_ref[g, pl.ds(start, both), :].astype(jnp.bfloat16) for g in range(groups)],
            axis=1,
        )
        if FLIP:
            res = jnp.dot(table_ref[...], x, preferred_element_type=jnp.float32).T
        else:
            res = lax.dot_general(
                x, table_ref[...], (((0,), (0,)), ((), ())), preferred_element_type=jnp.float32
            )
        out_ref[i] = jnp.where(place == i, 0.0, res).astype(out_ref.dtype)
        return carry

    lax.fori_loop(0, rows, lagged, 0, unroll=UNROLL2)


def correlate(first, second, table, offs):
    na, half, depth, rows = first.shape
    nb, _, _, wide = second.shape
    groups = 2 if nb % 2 == 0 else 1
    lags = table.shape[1]
    if FLIP:
        table = table.T
    spec = pltpu.PrefetchScalarGridSpec(
        num_scalar_prefetch=1,
        grid=(na, nb // groups),
        in_specs=[
            pl.BlockSpec((None, half, depth, rows), lambda i, j, o: (i, 0, 0, 0)),
            pl.BlockSpec((groups, half, depth, wide), lambda i, j, o: (j, 0, 0, 0)),
            pl.BlockSpec(table.shape, lambda i, j, o: (0, 0)),
        ],
        out_specs=pl.BlockSpec((rows, groups * wide, lags), lambda i, j, o: (i, j, 0)),
        scratch_shapes=[pltpu.VMEM((groups, rows * (2 * half + PAD), wide), jnp.float32)],
    )
    return pl.pallas_call(
        pair_kernel,
        grid_spec=spec,
        out_shape=jax.ShapeDtypeStruct((na * rows, nb * wide, lags), jnp.bfloat16),
        compiler_params=pltpu.CompilerParams(
            dimension_semantics=("arbitrary", "arbitrary"), vmem_limit_bytes=60 * 1024 * 1024
        ),
        name="pair_correlations",
    )(offs, first, second, table)


def by_lanes(parts):
    count, half, depth, owned = parts.shape
    if owned == LANES:
        return parts
    whole = parts.transpose(1, 2, 0, 3).reshape(half, depth, count * owned)
    lanes = math.gcd(LANES, count * owned)
    return whole.reshape(half, depth, -1, lanes).transpose(2, 0, 1, 3)


def local(rows, cols, raw_traces, channel_pick, clip_mask):
    owned = channel_pick.shape[0]
    windows = raw_traces.shape[1]
    samples = raw_traces.shape[2]
    half = samples // 2
    paired = raw_traces.reshape(owned, 2, windows, samples)
    parity = (channel_pick % 2)[:, None, None]
    picked = jnp.where(parity == 1, paired[:, 1], paired[:, 0])
    outgoing = whiten_block(picked, clip_mask)
    outgoing = outgoing.reshape(owned, windows, 2, half).transpose(3, 2, 1, 0)
    outgoing = outgoing.reshape(half, 2 * windows, owned)
    across = lax.ppermute(
        outgoing,
        ("row", "col"),
        [(c * cols + r, r * cols + c) for r in range(rows) for c in range(cols)],
    )
    second = lax.all_gather(across, "row", axis=0)
    first = lax.all_gather(outgoing, "col", axis=0)
    tile = owned * cols
    offs = jnp.stack([lax.axis_index("row") * tile, lax.axis_index("col") * tile])
    table = lag_table(half, samples, L, windows)
    return correlate(by_lanes(first), by_lanes(second), table, offs.astype(jnp.int32))


def solution(mesh):
    rows, cols = mesh.shape["row"], mesh.shape["col"]
    return jax.shard_map(
        functools.partial(local, rows, cols),
        mesh=mesh,
        in_specs=(
            P(("seg", "row", "col"), None, None),
            P(("seg", "row", "col")),
            P(("seg", "row", "col"), None),
        ),
        out_specs=P(("seg", "row"), "col", None),
        check_vma=False,
    )
```

```python
import functools
import math

import jax
import jax.numpy as jnp
from jax import lax
from jax.experimental import pallas as pl
from jax.experimental.pallas import tpu as pltpu
from jax.sharding import PartitionSpec as P

L = 128
LANES = 128
PAD = 8
UNROLL1 = 4
UNROLL2 = 4


def whiten_block(picked, keep):
    samples = picked.shape[2]
    half = samples // 2
    pos = jnp.arange(samples, dtype=jnp.int32)
    freq = jnp.arange(1, half + 1, dtype=jnp.int32)
    phase = pos[:, None] * freq[None, :] % samples
    angle = phase.astype(jnp.float32) * (2.0 * math.pi / samples)
    table = jnp.concatenate([jnp.cos(angle), -jnp.sin(angle)], axis=1)
    flat = picked.astype(jnp.float32).reshape(-1, samples)
    spec = jnp.dot(flat, table, precision=lax.Precision.HIGHEST, preferred_element_type=jnp.float32)
    real_part = spec[:, :half]
    imag_part = spec[:, half:]
    power = real_part * real_part + imag_part * imag_part
    gap = jnp.abs(freq[:, None] - freq[None, :])
    band = jnp.where(gap <= 2, 0.2, 0.0).astype(jnp.float32)
    smooth = jnp.dot(
        power, band, precision=lax.Precision.HIGHEST, preferred_element_type=jnp.float32
    )
    denom = jnp.sqrt(smooth + 0.1 * jnp.mean(power, axis=1, keepdims=True) + 1e-06)
    weight = keep.reshape(-1, 1).astype(jnp.float32) / denom
    whitened = jnp.concatenate([real_part * weight, imag_part * weight], axis=1)
    return whitened.astype(jnp.bfloat16).reshape(picked.shape[0], picked.shape[1], samples)


def lag_table(half, samples, lags, windows):
    freq = jnp.arange(1, half + 1, dtype=jnp.int32)
    shift = jnp.arange(lags, dtype=jnp.int32) - lags // 2
    phase = freq[:, None] * shift[None, :] % samples
    angle = phase.astype(jnp.float32) * (2.0 * math.pi / samples)
    scale = 1.0 / math.sqrt(windows * half)
    both = jnp.concatenate([jnp.cos(angle) * scale, -jnp.sin(angle) * scale], axis=0)
    return both.astype(jnp.bfloat16)


def pair_kernel(groups, offs_ref, first_ref, *refs):
    second_refs = refs[:groups]
    table_ref, out_ref, cross_ref = refs[groups], refs[-2], refs[-1]
    half, depth, rows = first_ref.shape
    wide = second_refs[0].shape[-1]
    both = 2 * half
    stride = both + PAD
    windows = depth // 2
    chunk = out_ref.shape[0]

    def spectra(k, carry):
        a = first_ref[k]
        turned = jnp.concatenate([a[windows:], -a[:windows]], axis=0)
        b = jnp.concatenate([ref[k] for ref in second_refs], axis=1)
        for part, lhs in enumerate((a, turned)):
            res = lax.dot_general(
                lhs, b, (((0,), (0,)), ((), ())), preferred_element_type=jnp.float32
            )
            for g in range(groups):
                cross_ref[g, pl.ds(part * half + k, rows, stride=stride), :] = res[
                    :, g * wide : (g + 1) * wide
                ]
        return carry

    @pl.when(pl.program_id(0) == 0)
    def _():
        lax.fori_loop(0, half, spectra, 0, unroll=UNROLL1)

    base = pl.program_id(0) * chunk
    swap = offs_ref[2]
    lags = table_ref.shape[0]
    gap = offs_ref[3] - base
    place = lax.broadcasted_iota(jnp.int32, (wide, lags), 0) + gap
    halves = [swap * wide, (1 - swap) * wide] if groups == 2 else [0]

    def lagged(i, carry):
        start = pl.multiple_of((base + i) * stride, 8)
        x = jnp.concatenate(
            [cross_ref[g, pl.ds(start, both), :].astype(jnp.bfloat16) for g in range(groups)],
            axis=1,
        )
        res = jnp.dot(table_ref[...], x, preferred_element_type=jnp.float32).T
        for g in range(groups):
            at = halves[g]
            piece = jnp.where(place + at == i, 0.0, res[g * wide : (g + 1) * wide])
            if groups == 2:
                at = pl.multiple_of(at, wide)
            out_ref[i, pl.ds(at, wide), :] = piece.astype(out_ref.dtype)
        return carry

    lax.fori_loop(0, chunk, lagged, 0, unroll=UNROLL2)


def correlate(prev, first, seconds, table, offs, shape):
    half, depth, rows = first.shape
    wide = seconds[0].shape[-1]
    groups = len(seconds)
    lags = table.shape[0]
    steps = 4 if rows % 4 == 0 else 1
    in_specs = [pl.BlockSpec((half, depth, rows), lambda i, o: (0, 0, 0))]
    in_specs += [pl.BlockSpec((half, depth, wide), lambda i, o: (0, 0, 0))] * groups
    in_specs += [pl.BlockSpec(table.shape, lambda i, o: (0, 0))]
    args = [offs, first, *seconds, table]
    aliases = {}
    if prev is not None:
        aliases = {len(args): 0}
        in_specs.append(pl.BlockSpec(memory_space=pl.ANY))
        args.append(prev)
    spec = pltpu.PrefetchScalarGridSpec(
        num_scalar_prefetch=1,
        grid=(steps,),
        in_specs=in_specs,
        out_specs=pl.BlockSpec(
            (rows // steps, groups * wide, lags), lambda i, o: (o[0] * steps + i, o[1], 0)
        ),
        scratch_shapes=[pltpu.VMEM((groups, rows * (2 * half + PAD), wide), jnp.float32)],
    )
    flops = 2 * rows * groups * wide * 2 * half * (depth + lags)
    return pl.pallas_call(
        functools.partial(pair_kernel, groups),
        grid_spec=spec,
        out_shape=jax.ShapeDtypeStruct(shape, jnp.bfloat16),
        input_output_aliases=aliases,
        cost_estimate=pl.CostEstimate(
            flops=8 * flops, bytes_accessed=2 * rows * groups * wide * lags, transcendentals=0
        ),
        compiler_params=pltpu.CompilerParams(
            dimension_semantics=("arbitrary",), vmem_limit_bytes=60 * 1024 * 1024
        ),
        name="pair_correlations",
    )(*args)


def by_lanes(parts):
    count, half, depth, owned = parts.shape
    whole = parts.transpose(1, 2, 0, 3).reshape(half, depth, count * owned)
    lanes = math.gcd(LANES, count * owned)
    return whole.reshape(half, depth, -1, lanes).transpose(2, 0, 1, 3)


def local(rows, cols, raw_traces, channel_pick, clip_mask):
    owned = channel_pick.shape[0]
    windows = raw_traces.shape[1]
    samples = raw_traces.shape[2]
    half = samples // 2
    paired = raw_traces.reshape(owned, 2, windows, samples)
    parity = (channel_pick % 2)[:, None, None]
    picked = jnp.where(parity == 1, paired[:, 1], paired[:, 0])
    outgoing = whiten_block(picked, clip_mask)
    outgoing = outgoing.reshape(owned, windows, 2, half).transpose(3, 2, 1, 0)
    outgoing = outgoing.reshape(half, 2 * windows, owned)
    across = lax.ppermute(
        outgoing,
        ("row", "col"),
        [(c * cols + r, r * cols + c) for r in range(rows) for c in range(cols)],
    )
    tile = owned * cols
    shape = (tile, tile, L)
    row, col = lax.axis_index("row"), lax.axis_index("col")
    ahead = (col - row) * tile
    table = lag_table(half, samples, L, windows).T
    prev = None

    def offsets(place, pair, swap, wide, lanes):
        gap = ahead + pair * wide - place * lanes
        return jnp.stack([jnp.int32(v) for v in (place, pair, swap, gap)])

    if owned != LANES or rows & (rows - 1) or rows < 2:
        firsts = by_lanes(lax.all_gather(outgoing, "col", axis=0))
        seconds = by_lanes(lax.all_gather(across, "row", axis=0))
        lanes = firsts.shape[-1]
        for i in range(firsts.shape[0]):
            for j in range(seconds.shape[0]):
                offs = offsets(i, j, 0, lanes, lanes)
                prev = correlate(prev, firsts[i], [seconds[j]], table, offs, shape)
        return prev

    def flipped(value, bit):
        return lax.ppermute(value, "row", [(r, r ^ bit) for r in range(rows)])

    def hop(value):
        return lax.ppermute(value, "col", [(c, (c + 1) % cols) for c in range(cols)])

    pairs = {0: (across, flipped(across, 1))}
    held, _ = lax.optimization_barrier((outgoing, across))
    firsts = {0: outgoing, 1: hop(held)} if cols > 1 else {0: outgoing}
    fars = {p: flipped(across, 2 * p) for p in range(1, rows // 2)}
    order = [(s, p) for s in range(cols) for p in range(rows // 2)]
    order.sort(key=lambda sp: (max(sp[0] // 2, sp[1]), sp[0] // 2, sp[1], sp[0]))
    ready = 1
    for step, (s, p) in enumerate(order):
        if step > 0:
            if p in fars and p not in pairs or step == 1 and fars:
                for q in [q for q in fars if q not in pairs][:1]:
                    prev, far = lax.optimization_barrier((prev, fars[q]))
                    pairs[q] = (far, flipped(far, 1))
            while p not in pairs:
                q = len(pairs)
                pairs[q] = (fars[q], flipped(fars[q], 1))
            if ready + 1 < cols and (step % 2 == 1 or s > ready):
                prev, last = lax.optimization_barrier((prev, firsts[ready]))
                ready += 1
                firsts[ready] = hop(last)
            while s > ready:
                ready += 1
                firsts[ready] = hop(firsts[ready - 1])
        place = (col - s) % cols
        other = row ^ (2 * p)
        offs = offsets(place, other // 2, other % 2, 2 * owned, owned)
        prev = correlate(prev, firsts[s], pairs[p], table, offs, shape)
    return prev


def solution(mesh):
    rows, cols = mesh.shape["row"], mesh.shape["col"]
    return jax.shard_map(
        functools.partial(local, rows, cols),
        mesh=mesh,
        in_specs=(
            P(("seg", "row", "col"), None, None),
            P(("seg", "row", "col")),
            P(("seg", "row", "col"), None),
        ),
        out_specs=P(("seg", "row"), "col", None),
        check_vma=False,
    )
```

```python
import functools
import math

import jax
import jax.numpy as jnp
from jax import lax
from jax.experimental import pallas as pl
from jax.experimental.pallas import tpu as pltpu
from jax.sharding import PartitionSpec as P

L = 128
LANES = 128
PAD = 8
UNROLL1 = 4
UNROLL2 = 4


def whiten_block(picked, keep):
    samples = picked.shape[2]
    half = samples // 2
    pos = jnp.arange(samples, dtype=jnp.int32)
    freq = jnp.arange(1, half + 1, dtype=jnp.int32)
    phase = pos[:, None] * freq[None, :] % samples
    angle = phase.astype(jnp.float32) * (2.0 * math.pi / samples)
    table = jnp.concatenate([jnp.cos(angle), -jnp.sin(angle)], axis=1)
    flat = picked.astype(jnp.float32).reshape(-1, samples)
    spec = jnp.dot(flat, table, precision=lax.Precision.HIGHEST, preferred_element_type=jnp.float32)
    real_part = spec[:, :half]
    imag_part = spec[:, half:]
    power = real_part * real_part + imag_part * imag_part
    gap = jnp.abs(freq[:, None] - freq[None, :])
    band = jnp.where(gap <= 2, 0.2, 0.0).astype(jnp.float32)
    smooth = jnp.dot(
        power, band, precision=lax.Precision.HIGHEST, preferred_element_type=jnp.float32
    )
    denom = jnp.sqrt(smooth + 0.1 * jnp.mean(power, axis=1, keepdims=True) + 1e-06)
    weight = keep.reshape(-1, 1).astype(jnp.float32) / denom
    whitened = jnp.concatenate([real_part * weight, imag_part * weight], axis=1)
    return whitened.astype(jnp.bfloat16).reshape(picked.shape[0], picked.shape[1], samples)


def lag_table(half, samples, lags, windows):
    freq = jnp.arange(1, half + 1, dtype=jnp.int32)
    shift = jnp.arange(lags, dtype=jnp.int32) - lags // 2
    phase = freq[:, None] * shift[None, :] % samples
    angle = phase.astype(jnp.float32) * (2.0 * math.pi / samples)
    scale = 1.0 / math.sqrt(windows * half)
    both = jnp.concatenate([jnp.cos(angle) * scale, -jnp.sin(angle) * scale], axis=0)
    return both.astype(jnp.bfloat16)


def pair_kernel(groups, offs_ref, first_ref, *refs):
    second_refs = refs[:groups]
    table_ref, out_ref, cross_ref = refs[groups], refs[-2], refs[-1]
    half, depth, rows = first_ref.shape
    wide = second_refs[0].shape[-1]
    both = 2 * half
    stride = both + PAD
    windows = depth // 2
    chunk = out_ref.shape[0]

    def spectra(k, carry):
        a = first_ref[k]
        turned = jnp.concatenate([a[windows:], -a[:windows]], axis=0)
        b = jnp.concatenate([ref[k] for ref in second_refs], axis=1)
        for part, lhs in enumerate((a, turned)):
            res = lax.dot_general(
                lhs, b, (((0,), (0,)), ((), ())), preferred_element_type=jnp.float32
            )
            for g in range(groups):
                cross_ref[g, pl.ds(part * half + k, rows, stride=stride), :] = res[
                    :, g * wide : (g + 1) * wide
                ]
        return carry

    @pl.when(pl.program_id(0) == 0)
    def _():
        lax.fori_loop(0, half, spectra, 0, unroll=UNROLL1)

    base = pl.program_id(0) * chunk
    swap = offs_ref[2]
    lags = table_ref.shape[0]
    gap = offs_ref[3] - base
    place = lax.broadcasted_iota(jnp.int32, (wide, lags), 0) + gap
    halves = [swap * wide, (1 - swap) * wide] if groups == 2 else [0]

    def lagged(i, carry):
        start = pl.multiple_of((base + i) * stride, 8)
        x = jnp.concatenate(
            [cross_ref[g, pl.ds(start, both), :].astype(jnp.bfloat16) for g in range(groups)],
            axis=1,
        )
        res = jnp.dot(table_ref[...], x, preferred_element_type=jnp.float32).T
        for g in range(groups):
            at = halves[g]
            piece = jnp.where(place + at == i, 0.0, res[g * wide : (g + 1) * wide])
            if groups == 2:
                at = pl.multiple_of(at, wide)
            out_ref[i, pl.ds(at, wide), :] = piece.astype(out_ref.dtype)
        return carry

    lax.fori_loop(0, chunk, lagged, 0, unroll=UNROLL2)


def correlate(prev, first, seconds, table, offs, shape):
    half, depth, rows = first.shape
    wide = seconds[0].shape[-1]
    groups = len(seconds)
    lags = table.shape[0]
    steps = 4 if rows % 4 == 0 else 1
    in_specs = [pl.BlockSpec((half, depth, rows), lambda i, o: (0, 0, 0))]
    in_specs += [pl.BlockSpec((half, depth, wide), lambda i, o: (0, 0, 0))] * groups
    in_specs += [pl.BlockSpec(table.shape, lambda i, o: (0, 0))]
    args = [offs, first, *seconds, table]
    aliases = {}
    if prev is not None:
        aliases = {len(args): 0}
        in_specs.append(pl.BlockSpec(memory_space=pl.ANY))
        args.append(prev)
    spec = pltpu.PrefetchScalarGridSpec(
        num_scalar_prefetch=1,
        grid=(steps,),
        in_specs=in_specs,
        out_specs=pl.BlockSpec(
            (rows // steps, groups * wide, lags), lambda i, o: (o[0] * steps + i, o[1], 0)
        ),
        scratch_shapes=[pltpu.VMEM((groups, rows * (2 * half + PAD), wide), jnp.float32)],
    )
    flops = 2 * rows * groups * wide * 2 * half * (depth + lags)
    return pl.pallas_call(
        functools.partial(pair_kernel, groups),
        grid_spec=spec,
        out_shape=jax.ShapeDtypeStruct(shape, jnp.bfloat16),
        input_output_aliases=aliases,
        cost_estimate=pl.CostEstimate(
            flops=8 * flops, bytes_accessed=2 * rows * groups * wide * lags, transcendentals=0
        ),
        compiler_params=pltpu.CompilerParams(
            dimension_semantics=("arbitrary",), vmem_limit_bytes=60 * 1024 * 1024
        ),
        name="pair_correlations",
    )(*args)


def by_lanes(parts):
    count, half, depth, owned = parts.shape
    whole = parts.transpose(1, 2, 0, 3).reshape(half, depth, count * owned)
    lanes = math.gcd(LANES, count * owned)
    return whole.reshape(half, depth, -1, lanes).transpose(2, 0, 1, 3)


def local(rows, cols, raw_traces, channel_pick, clip_mask):
    owned = channel_pick.shape[0]
    windows = raw_traces.shape[1]
    samples = raw_traces.shape[2]
    half = samples // 2
    paired = raw_traces.reshape(owned, 2, windows, samples)
    parity = (channel_pick % 2)[:, None, None]
    picked = jnp.where(parity == 1, paired[:, 1], paired[:, 0])
    outgoing = whiten_block(picked, clip_mask)
    outgoing = outgoing.reshape(owned, windows, 2, half).transpose(3, 2, 1, 0)
    outgoing = outgoing.reshape(half, 2 * windows, owned)
    tile = owned * cols
    shape = (tile, tile, L)
    row, col = lax.axis_index("row"), lax.axis_index("col")
    ahead = (col - row) * tile
    table = lag_table(half, samples, L, windows).T
    prev = None

    def offsets(place, pair, swap, wide, lanes):
        gap = ahead + pair * wide - place * lanes
        return jnp.stack([jnp.int32(v) for v in (place, pair, swap, gap)])

    if owned != LANES or rows & (rows - 1) or rows < 2 or rows != cols:
        across = lax.ppermute(
            outgoing,
            ("row", "col"),
            [(c * cols + r, r * cols + c) for r in range(rows) for c in range(cols)],
        )
        firsts = by_lanes(lax.all_gather(outgoing, "col", axis=0))
        seconds = by_lanes(lax.all_gather(across, "row", axis=0))
        lanes = firsts.shape[-1]
        for i in range(firsts.shape[0]):
            for j in range(seconds.shape[0]):
                offs = offsets(i, j, 0, lanes, lanes)
                prev = correlate(prev, firsts[i], [seconds[j]], table, offs, shape)
        return prev

    def flipped(value, bit):
        return lax.ppermute(value, "row", [(r, r ^ bit) for r in range(rows)])

    def hop(value):
        return lax.ppermute(value, "col", [(c, (c + 1) % cols) for c in range(cols)])

    def brought(near, source):
        found = None
        for away in range(rows // 2):
            moves = []
            for c in range(cols):
                for q in (2 * ((c // 2) ^ near), 2 * ((c // 2) ^ near) + 1):
                    target = 2 * ((c // 2) ^ away) + q % 2
                    moves.append((c * cols + q, target * cols + c))
            here = lax.ppermute(source, ("row", "col"), moves)
            mine = (row // 2) ^ (col // 2) == away
            found = here if found is None else jnp.where(mine, here, found)
        return found

    near = brought(0, outgoing)
    pairs = {0: (near, flipped(near, 1))}
    held, _ = lax.optimization_barrier((outgoing, near))
    firsts = {0: outgoing, 1: hop(held)} if cols > 1 else {0: outgoing}
    fars = {p: brought(p, held) for p in range(1, rows // 2)}
    order = [(s, p) for s in range(cols) for p in range(rows // 2)]
    order.sort(key=lambda sp: (sp[0] // 3, sp[1], sp[0]))
    ready = 1
    for step, (s, p) in enumerate(order):
        if step > 0:
            if p in fars and p not in pairs or step == 2 and fars:
                for q in [q for q in fars if q not in pairs][:1]:
                    prev, far = lax.optimization_barrier((prev, fars[q]))
                    pairs[q] = (far, flipped(far, 1))
            while p not in pairs:
                q = len(pairs)
                pairs[q] = (fars[q], flipped(fars[q], 1))
            if ready + 1 < cols and (step % 2 == 1 or s > ready):
                prev, last = lax.optimization_barrier((prev, firsts[ready]))
                ready += 1
                firsts[ready] = hop(last)
            while s > ready:
                ready += 1
                firsts[ready] = hop(firsts[ready - 1])
        place = (col - s) % cols
        offs = offsets(place, (col // 2) ^ p, row % 2, 2 * owned, owned)
        prev = correlate(prev, firsts[s], pairs[p], table, offs, shape)
    return prev


def solution(mesh):
    rows, cols = mesh.shape["row"], mesh.shape["col"]
    return jax.shard_map(
        functools.partial(local, rows, cols),
        mesh=mesh,
        in_specs=(
            P(("seg", "row", "col"), None, None),
            P(("seg", "row", "col")),
            P(("seg", "row", "col"), None),
        ),
        out_specs=P(("seg", "row"), "col", None),
        check_vma=False,
    )
```
